512 devices in a mesh: frame: 32 (over z, x), tile: 16 (over y, core).
Axes of the slice: x: 4, y: 8, z: 8, core: 2. Of those that a mesh axis runs over, the one named last changes fastest.
Arguments:
- frames: bfloat16 [32, 3, 64, 256, 256], P('frame', None, None, 'tile'), may hold values from -6 to 6
- state_in: bfloat16 [32, 64, 256, 256], P('frame', None, 'tile'), may hold values from -6 to 6
- motion: int32 [3, 32, 3, 256], replicated, may hold values from -4 to 255, as said below
- merge_w: bfloat16 [64, 1152], replicated, may hold values from -0.1875 to 0.1875
- res_w: bfloat16 [1, 2, 64, 576], replicated, may hold values from -0.25 to 0.25
Outputs:
- states: bfloat16 [32, 3, 64, 256, 256], P('frame', None, None, 'tile')
The draws below stay inside these ranges and needn't reach their ends.
Inputs may be any that keep to these rules, and one draw needn't show every extreme that they name: motion[0] names a source block of the same frame; blocks t * 16 to t * 16 + 15 form tile owner t. For each section, tick and owner, at most 2 of the owner's 16 destination blocks read blocks of any one owner, and exactly 2 read one owner. motion[1] and motion[2] lie in -4 to 4.
All inputs are finite; a program needn't handle non-finite values.
Results may differ from the reference program's by a relative error of at most 0.0095.
Values may be sent and summed in bfloat16 or wider, within the bound.
A program may use at most 64 MiB of HBM per device.

```python
import jax
import jax.numpy as jnp
from jax import lax

C = 64
BH = 8
BW = 32
OFF = 4
TICKS = 3
RB = 1
TPD = 16
CAP = 2
TILES = 256
N_FRAME = 32
N_TILE = 16


def draw_motion(key, part):
    base_key = jax.random.fold_in(key, 7)
    k_first, k_pool, k_order, k_block, k_down, k_right = jax.random.split(base_key, 6)
    row_count = N_FRAME * TICKS * N_TILE
    pool_width = (N_TILE - 1) * CAP
    first_owner = jax.random.randint(k_first, (row_count, 1), 0, N_TILE, dtype=jnp.int32)
    others = (first_owner + 1 + jnp.arange(pool_width, dtype=jnp.int32)[None, :] // CAP) % N_TILE
    scores = jax.random.randint(k_pool, (row_count, pool_width), 0, 1 << 20, dtype=jnp.int32) * pool_width + jnp.arange(pool_width, dtype=jnp.int32)[None, :]
    pool_order = jnp.argsort(scores, axis=1)
    picked = jnp.take_along_axis(others, pool_order, axis=1)[:, :TPD - CAP]
    owners = jnp.concatenate([jnp.broadcast_to(first_owner, (row_count, CAP)), picked], axis=1)
    mixing = jax.random.randint(k_order, (row_count, TPD), 0, 1 << 20, dtype=jnp.int32) * TPD + jnp.arange(TPD, dtype=jnp.int32)[None, :]
    owners = jnp.take_along_axis(owners, jnp.argsort(mixing, axis=1), axis=1)
    local_block = jax.random.randint(k_block, (row_count, TPD), 0, TPD, dtype=jnp.int32)
    source = (owners * TPD + local_block).reshape(N_FRAME, TICKS, N_TILE * TPD)
    down_by = jax.random.randint(k_down, (N_FRAME, TICKS, N_TILE * TPD), -OFF, OFF + 1, dtype=jnp.int32)
    right_by = jax.random.randint(k_right, (N_FRAME, TICKS, N_TILE * TPD), -OFF, OFF + 1, dtype=jnp.int32)
    return jnp.stack([source, down_by, right_by]).astype(jnp.int32)


def level_of(key, extent, cuts, low, top_value):
    def one(axis_at, shards_of):
        steps = jax.random.uniform(jax.random.fold_in(jax.random.fold_in(key, 6), axis_at), (shards_of,), jnp.float32, low / len(cuts), top_value / len(cuts))
        return jnp.repeat(jnp.exp(steps), extent[axis_at] // shards_of).reshape((-1,) + (1,) * (len(extent) - axis_at - 1))

    factor_of = one(*cuts[0])
    for cut in cuts[1:]:
        factor_of = factor_of * one(*cut)
    return factor_of


def normal_values(stream_key, shape, deviation, limit, cuts=(), kind=jnp.bfloat16):
    values = deviation * jax.random.normal(stream_key, shape, jnp.float32)
    if cuts:
        values = values * level_of(stream_key, shape, cuts, -0.22, 0.18)
    return jnp.clip(values, -limit, limit).astype(kind)


def setup_inputs(seed: int = 0) -> dict:
    seeds = jax.random.split(jax.random.key(seed), 6)
    return {
        "frames": normal_values(seeds[0], (N_FRAME, TICKS, C, TILES, BH * BW), 1.0, 6.0, ((0, 32), (3, 16))),
        "state_in": normal_values(seeds[1], (N_FRAME, C, TILES, BH * BW), 1.0, 6.0, ((0, 32), (2, 16))),
        "motion": draw_motion(jax.random.fold_in(seeds[5], 71), 0),
        "merge_w": normal_values(seeds[3], (C, 18 * C), (18 * C) ** -0.5, 0.1875),
        "res_w": normal_values(seeds[4], (RB, 2, C, 9 * C), (9 * C) ** -0.5, 0.25),
    }


def displace(field, down_by, right_by, keep):
    pixels = field.shape[-1]
    padding = OFF * (BW + 1)
    widths = [(0, 0)] * (field.ndim - 1) + [(padding, padding)]
    padded = jnp.pad(field, widths)
    window = lax.dynamic_slice_in_dim(padded, padding + down_by * BW + right_by, pixels, field.ndim - 1)
    places = jnp.arange(pixels, dtype=jnp.int32)
    row_at = places // BW + down_by
    col_at = places % BW + right_by
    inside = (row_at >= 0) & (row_at < pixels // BW) & (col_at >= 0) & (col_at < BW) & keep
    return jnp.where(inside, window, jnp.zeros_like(window))


def convolve(field, kernel):
    in_width, count, pixels = field.shape
    taps = [displace(field, row_step, col_step, True) for row_step in (-1, 0, 1) for col_step in (-1, 0, 1)]
    stacked = jnp.stack(taps).reshape(9 * in_width, count * pixels)
    result = jnp.dot(kernel, stacked, preferred_element_type=jnp.float32)
    return result.reshape(kernel.shape[0], count, pixels)


def advance(warped, frame_now, merge_w, res_w):
    joined = jnp.concatenate([frame_now, warped], axis=0)
    merged = convolve(joined, merge_w)
    merged = jnp.where(merged > 0, merged, 0.1 * merged).astype(jnp.bfloat16)
    hidden = merged
    for layer_index in range(res_w.shape[0]):
        middle = jax.nn.relu(convolve(hidden, res_w[layer_index, 0])).astype(jnp.bfloat16)
        hidden = (hidden.astype(jnp.float32) + convolve(middle, res_w[layer_index, 1])).astype(jnp.bfloat16)
    return hidden


def one_section(packed):
    previous, frame_now, columns, merge_w, res_w = packed
    blocks = jnp.take(previous, columns[0], axis=1)
    warped = jax.vmap(displace, in_axes=(1, 0, 0, None), out_axes=1)(blocks, columns[1], columns[2], True)
    return advance(warped, frame_now, merge_w, res_w)


def reference(frames, state_in, motion, merge_w, res_w):
    previous = state_in
    outputs = []
    for tick_index in range(TICKS):
        columns = jnp.transpose(motion[:, :, tick_index, :], (1, 0, 2))

        def section_work(packed):
            return one_section((packed[0], packed[1], packed[2], merge_w, res_w))

        produced = lax.map(section_work, (previous, frames[:, tick_index], columns))
        outputs.append(produced)
        previous = jnp.roll(produced, 1, axis=0)
    return jnp.stack(outputs, axis=1)
```

```python
import functools

import jax
import jax.numpy as jnp
from jax import lax
from jax.experimental import pallas as pl
from jax.experimental.pallas import tpu as pltpu
from jax.sharding import PartitionSpec as P

BW = 32
MESH = pl.DeviceIdType.MESH
F32, BF16 = jnp.float32, jnp.bfloat16
BATCHES = 4


def row_taps(halves, lane):
    low, high = halves
    down_low, down_high = pltpu.roll(low, BW, 1), pltpu.roll(high, BW, 1)
    up_low, up_high = pltpu.roll(low, 128 - BW, 1), pltpu.roll(high, 128 - BW, 1)
    first, last = lane < BW, lane >= 128 - BW
    zero = jnp.zeros_like(low)
    left = jnp.concatenate(
        [jnp.where(first, zero, down_low), low, jnp.where(last, up_high, up_low)], axis=0
    )
    right = jnp.concatenate(
        [jnp.where(first, down_low, down_high), high, jnp.where(last, zero, up_high)], axis=0
    )
    return jnp.concatenate([left.astype(BF16), right.astype(BF16)], axis=1)


def column_sum(product, width, col):
    halves = []
    for half in range(2):
        part = product[:, 128 * half : 128 * half + 128]
        before = jnp.where(col > 0, pltpu.roll(part[:width], 1, 1), 0.0)
        after = jnp.where(col < BW - 1, pltpu.roll(part[2 * width :], 127, 1), 0.0)
        halves.append(before + part[width : 2 * width] + after)
    return halves


def kernel(
    tiles, sections, ticks, motion_ref, first_ref, frames_ref, weight_ref, out_ref,
    moves, pieces, held_0, held_1, held_2, picked, arrived, part,
    moves_sem, one_send, one_recv, two_send, two_recv,
):
    held = (held_0, held_1, held_2)
    section = lax.axis_index("frame")
    owner = lax.axis_index("tile")
    ahead = lax.rem(section + 1, sections)
    behind = lax.rem(section + sections - 1, sections)
    per_owner = pieces.shape[2]
    width = out_ref.shape[2]
    span = per_owner // BATCHES

    moves_copy = pltpu.make_async_copy(motion_ref.at[:, section], moves, moves_sem)
    moves_copy.start()

    barrier = pltpu.get_barrier_semaphore()

    @pl.loop(1, tiles)
    def _(step):
        pl.semaphore_signal(
            barrier, inc=1, device_id={"tile": lax.rem(owner + step, tiles)}, device_id_type=MESH
        )

    @pl.loop(0, tiles)
    def _(step):
        pl.semaphore_signal(
            barrier, inc=1, device_id={"frame": behind, "tile": step}, device_id_type=MESH
        )

    pl.semaphore_wait(barrier, 2 * tiles - 1)

    def partner(step):
        turn = (step + 1) // 2 * (1 - 2 * lax.rem(step, 2))
        return lax.rem(owner + tiles // 2 + turn + tiles, tiles)

    def spread(source, target, send_sem, recv_sem):
        @pl.loop(0, tiles)
        def _(step):
            other = partner(step)

            @pl.when(other != owner)
            def _():
                pltpu.make_async_remote_copy(
                    src_ref=source(other), dst_ref=target, send_sem=send_sem, recv_sem=recv_sem,
                    device_id={"tile": other}, device_id_type=MESH,
                ).start()

            @pl.when(other == owner)
            def _():
                pltpu.make_async_copy(source(other), target, recv_sem).start()

    lane = lax.broadcasted_iota(jnp.int32, (width, 128), 1)
    col = lax.rem(lane, BW)
    pixels = 8 * BW
    place = lax.broadcasted_iota(jnp.int32, (1, pixels), 1)
    row_id = lax.broadcasted_iota(jnp.int32, (pixels, pixels), 0)

    spread(
        lambda other: first_ref.at[other], held[0].at[owner], one_send.at[0], one_recv.at[0]
    )

    for tick in range(ticks):
        def frame_part(block, carry, tick=tick):
            value = frames_ref[tick, block].astype(F32)
            part[block] = jnp.dot(
                weight_ref[0],
                row_taps((value[:, :128], value[:, 128:]), lane),
                preferred_element_type=F32,
            )
            return carry

        lax.fori_loop(0, per_owner, frame_part, 0)

        if tick == 0:
            moves_copy.wait()
        pltpu.make_async_copy(held[tick], held[tick], one_recv.at[tick]).wait()

        for batch in range(BATCHES):
            def pick(dest, carry, tick=tick, batch=batch):
                for local in range(span):
                    slot = batch * span + local
                    source = moves[0, tick, dest * per_owner + slot]
                    picked[tick, dest, slot] = held[tick][
                        source // per_owner, lax.rem(source, per_owner)
                    ]
                return carry

            lax.fori_loop(0, tiles, pick, 0)
            group = pl.ds(batch * span, span)
            spread(
                lambda other: picked.at[tick, other, group],
                arrived.at[tick, owner, group],
                two_send.at[tick, batch],
                two_recv.at[tick, batch],
            )

        for batch in range(BATCHES):
            group = pl.ds(batch * span, span)
            landed = arrived.at[tick, :, group]
            pltpu.make_async_copy(landed, landed, two_recv.at[tick, batch]).wait()

            def one_block(local, carry, tick=tick, batch=batch):
                block = batch * span + local
                down_by = moves[1, tick, owner * per_owner + block]
                right_by = moves[2, tick, owner * per_owner + block]
                row_at, col_at = place // BW + down_by, lax.rem(place, BW) + right_by
                inside = (row_at >= 0) & (row_at < 8) & (col_at >= 0) & (col_at < BW)
                wanted = jnp.where(inside, row_at * BW + col_at, -1)
                table = jnp.where(row_id == wanted, 1.0, 0.0).astype(BF16)
                value = jnp.concatenate(
                    [
                        jnp.concatenate(
                            [
                                arrived[tick, 2 * i + j, block].astype(F32)
                                for i in range(width // 8)
                            ],
                            axis=0,
                        )
                        for j in range(2)
                    ],
                    axis=1,
                ).astype(BF16)
                warped = jnp.dot(value, table, preferred_element_type=F32)
                product = part[block] + jnp.dot(
                    weight_ref[1],
                    row_taps((warped[:, :128], warped[:, 128:]), lane),
                    preferred_element_type=F32,
                )
                merged = [
                    jnp.where(half > 0, half, 0.1 * half).astype(BF16).astype(F32)
                    for half in column_sum(product, width, col)
                ]
                product = jnp.dot(
                    weight_ref[2], row_taps(merged, lane), preferred_element_type=F32
                )
                middle = [
                    jnp.maximum(half, 0.0).astype(BF16).astype(F32)
                    for half in column_sum(product, width, col)
                ]
                product = jnp.dot(
                    weight_ref[3], row_taps(middle, lane), preferred_element_type=F32
                )
                added = column_sum(product, width, col)
                for j in range(2):
                    hidden = merged[j] + added[j]
                    out_ref[tick, block, :, 128 * j : 128 * j + 128] = hidden.astype(BF16)
                    if tick + 1 < ticks:
                        for i in range(width // 8):
                            pieces[tick, 2 * i + j, block] = hidden[8 * i : 8 * i + 8].astype(BF16)
                return carry

            lax.fori_loop(0, span, one_block, 0)

            if tick + 1 < ticks:
                @pl.loop(0, tiles)
                def _(step, tick=tick, group=group):
                    other = partner(step)
                    pltpu.make_async_remote_copy(
                        src_ref=pieces.at[tick, other, group],
                        dst_ref=held[tick + 1].at[owner, group],
                        send_sem=one_send.at[tick + 1],
                        recv_sem=one_recv.at[tick + 1],
                        device_id={"frame": ahead, "tile": other},
                        device_id_type=MESH,
                    ).start()

    sent = first_ref.at[pl.ds(0, tiles - 1)]
    pltpu.make_async_copy(sent, sent, one_send.at[0]).wait()
    for tick in range(ticks):
        if tick + 1 < ticks:
            sent = pieces.at[tick]
            pltpu.make_async_copy(sent, sent, one_send.at[tick + 1]).wait()
        for batch in range(BATCHES):
            sent = picked.at[tick, pl.ds(0, tiles - 1), pl.ds(batch * span, span)]
            pltpu.make_async_copy(sent, sent, two_send.at[tick, batch]).wait()


def stacked_weight(weight):
    out_width, columns = weight.shape
    taps = weight.reshape(out_width, 3, 3, columns // 9)
    return jnp.transpose(taps, (2, 0, 1, 3))


def per_device(frames, state_in, motion, merge_w, res_w, tiles, sections):
    ticks, width, per_owner, pixels = frames.shape[1:]
    first = state_in[0].reshape(width // 8, 8, per_owner, 2, 128)
    first = jnp.transpose(first, (0, 3, 2, 1, 4)).reshape(tiles, per_owner, 8, 128)
    blocks = jnp.transpose(frames[0], (0, 2, 1, 3))
    merge = stacked_weight(merge_w)
    weight = jnp.stack(
        [
            merge[..., :width], merge[..., width:],
            stacked_weight(res_w[0, 0]), stacked_weight(res_w[0, 1]),
        ]
    ).reshape(4, 3 * width, 3 * width)
    vmem = pl.BlockSpec(memory_space=pltpu.VMEM)
    piece = (per_owner, 8, 128)
    out = pl.pallas_call(
        functools.partial(kernel, tiles, sections, ticks),
        out_shape=jax.ShapeDtypeStruct((ticks, per_owner, width, pixels), BF16),
        in_specs=[pl.BlockSpec(memory_space=pl.ANY), vmem, vmem, vmem],
        out_specs=vmem,
        scratch_shapes=[
            pltpu.SMEM((3, ticks, tiles * per_owner), jnp.int32),
            pltpu.VMEM((ticks - 1, tiles) + piece, BF16),
            pltpu.VMEM((tiles,) + piece, BF16),
            pltpu.VMEM((tiles,) + piece, BF16),
            pltpu.VMEM((tiles,) + piece, BF16),
            pltpu.VMEM((ticks, tiles) + piece, BF16),
            pltpu.VMEM((ticks, tiles) + piece, BF16),
            pltpu.VMEM((per_owner, 3 * width, pixels), F32),
            pltpu.SemaphoreType.DMA(()),
            pltpu.SemaphoreType.DMA((ticks,)),
            pltpu.SemaphoreType.DMA((ticks,)),
            pltpu.SemaphoreType.DMA((ticks, BATCHES)),
            pltpu.SemaphoreType.DMA((ticks, BATCHES)),
        ],
        compiler_params=pltpu.CompilerParams(
            collective_id=0, has_side_effects=True, vmem_limit_bytes=40 << 20
        ),
    )(motion, first, blocks, weight)
    return jnp.transpose(out, (0, 2, 1, 3))[None]


def solution(mesh):
    placed = (P("frame", None, None, "tile", None), P("frame", None, "tile", None), P(), P(), P())
    body = functools.partial(
        per_device, tiles=mesh.shape["tile"], sections=mesh.shape["frame"]
    )
    return jax.shard_map(
        body,
        mesh=mesh,
        in_specs=placed,
        out_specs=P("frame", None, None, "tile", None),
        check_vma=False,
    )
```

```python
import functools

import jax
import jax.numpy as jnp
from jax import lax
from jax.experimental import pallas as pl
from jax.experimental.pallas import tpu as pltpu
from jax.sharding import PartitionSpec as P

BW = 32
MESH = pl.DeviceIdType.MESH
F32, BF16 = jnp.float32, jnp.bfloat16
BATCHES = 4
TOGETHER = 4


def row_taps(halves, lane):
    low, high = halves
    down_low, down_high = pltpu.roll(low, BW, 1), pltpu.roll(high, BW, 1)
    up_low, up_high = pltpu.roll(low, 128 - BW, 1), pltpu.roll(high, 128 - BW, 1)
    first, last = lane < BW, lane >= 128 - BW
    zero = jnp.zeros_like(low)
    left = jnp.concatenate(
        [jnp.where(first, zero, down_low), low, jnp.where(last, up_high, up_low)], axis=0
    )
    right = jnp.concatenate(
        [jnp.where(first, down_low, down_high), high, jnp.where(last, zero, up_high)], axis=0
    )
    return jnp.concatenate([left, right], axis=1)


def column_sum(product, width, col):
    halves = []
    for half in range(2):
        part = product[:, 128 * half : 128 * half + 128]
        before = jnp.where(col > 0, pltpu.roll(part[:width], 1, 1), 0.0)
        after = jnp.where(col < BW - 1, pltpu.roll(part[2 * width :], 127, 1), 0.0)
        halves.append(before + part[width : 2 * width] + after)
    return halves


def kernel(
    tiles, sections, ticks, motion_ref, first_ref, frames_ref, merge_ref, weight_ref, out_ref,
    moves, pieces, held_0, held_1, held_2, picked, arrived, part,
    moves_sem, one_send, one_recv, two_send, two_recv,
):
    held = (held_0, held_1, held_2)
    section = lax.axis_index("frame")
    owner = lax.axis_index("tile")
    ahead = lax.rem(section + 1, sections)
    behind = lax.rem(section + sections - 1, sections)
    per_owner = pieces.shape[2]
    width = out_ref.shape[2]
    span = per_owner // BATCHES

    moves_copy = pltpu.make_async_copy(motion_ref.at[:, section], moves, moves_sem)
    moves_copy.start()

    barrier = pltpu.get_barrier_semaphore()

    @pl.loop(1, tiles)
    def _(step):
        pl.semaphore_signal(
            barrier, inc=1, device_id={"tile": lax.rem(owner + step, tiles)}, device_id_type=MESH
        )

    @pl.loop(0, tiles)
    def _(step):
        pl.semaphore_signal(
            barrier, inc=1, device_id={"frame": behind, "tile": step}, device_id_type=MESH
        )

    pl.semaphore_wait(barrier, 2 * tiles - 1)

    order = sorted(range(1, tiles), key=lambda step: -min(step, tiles - step))

    def other_at(step):
        return lax.rem(owner + step, tiles)

    lane = lax.broadcasted_iota(jnp.int32, (width, 128), 1)
    col = lax.rem(lane, BW)

    mine = pl.ds(owner * per_owner, per_owner)
    for step in order:
        other = other_at(step)
        pltpu.make_async_remote_copy(
            src_ref=first_ref.at[other], dst_ref=held[0].at[mine],
            send_sem=one_send.at[0], recv_sem=one_recv.at[0],
            device_id={"tile": other}, device_id_type=MESH,
        ).start()
    held[0][mine] = first_ref[owner]

    def frame_taps(turn, carry):
        for tick in range(ticks):
            value = frames_ref[tick, turn]
            part[tick, turn] = row_taps((value[:, :128], value[:, 128:]), lane)
        return carry

    lax.fori_loop(0, per_owner, frame_taps, 0)

    for tick in range(ticks):
        if tick == 0:
            moves_copy.wait()
        landed = held[tick].at[pl.ds(0, (tiles - (tick == 0)) * per_owner)]
        pltpu.make_async_copy(landed, landed, one_recv.at[tick]).wait()

        for batch in range(BATCHES):
            group = pl.ds(batch * span, span)
            for step in order + [0]:
                other = other_at(step)
                for slot in range(batch * span, batch * span + span):
                    value = held[tick][moves[0, tick, other * per_owner + slot]]
                    if step:
                        picked[tick, other, slot] = value
                    else:
                        arrived[tick, owner, slot] = value
                if step:
                    pltpu.make_async_remote_copy(
                        src_ref=picked.at[tick, other, group],
                        dst_ref=arrived.at[tick, owner, group],
                        send_sem=two_send.at[tick, batch], recv_sem=two_recv.at[tick, batch],
                        device_id={"tile": other}, device_id_type=MESH,
                    ).start()

        for batch in range(BATCHES):
            group = pl.ds(batch * span, span)
            landed = arrived.at[tick, pl.ds(0, tiles - 1), group]
            pltpu.make_async_copy(landed, landed, two_recv.at[tick, batch]).wait()

            def some_blocks(turn, carry, tick=tick, batch=batch):
                blocks = [batch * span + turn * TOGETHER + local for local in range(TOGETHER)]

                def displaced(block):
                    down_by = moves[1, tick, owner * per_owner + block]
                    right_by = moves[2, tick, owner * per_owner + block]
                    offset = down_by * BW + right_by
                    col_at = col + right_by
                    turned = [
                        pltpu.roll(
                            jnp.concatenate(
                                [
                                    arrived[tick, 2 * i + j, block].astype(F32)
                                    for i in range(width // 8)
                                ],
                                axis=0,
                            ),
                            lax.rem(3 * 128 - offset, 128),
                            1,
                        ).astype(BF16)
                        for j in range(2)
                    ]
                    halves = []
                    for j in range(2):
                        source = lane + (128 * j + offset)
                        column = (col_at >= 0) & (col_at < BW)
                        from_low = column & (source >= 0) & (source < 128)
                        from_high = column & (source >= 128) & (source < 256)
                        rest = jnp.where(from_high, turned[1], jnp.zeros_like(turned[1]))
                        halves.append(jnp.where(from_low, turned[0], rest))
                    return halves

                def convolved(index, halves):
                    return jnp.dot(
                        weight_ref[index], row_taps(halves, lane), preferred_element_type=F32
                    )

                def merging(block, halves):
                    return jnp.dot(
                        merge_ref[...],
                        jnp.concatenate([part[tick, block], row_taps(halves, lane)], axis=0),
                        preferred_element_type=F32,
                    )

                values = [displaced(block) for block in blocks]
                merged = [
                    [
                        jnp.where(half > 0, half, 0.1 * half).astype(BF16)
                        for half in column_sum(merging(block, halves), width, col)
                    ]
                    for block, halves in zip(blocks, values)
                ]
                middle = [
                    [
                        jnp.maximum(half, 0.0).astype(BF16)
                        for half in column_sum(convolved(0, halves), width, col)
                    ]
                    for halves in merged
                ]
                for block, before, halves in zip(blocks, merged, middle):
                    added = column_sum(convolved(1, halves), width, col)
                    for j in range(2):
                        hidden = before[j].astype(F32) + added[j]
                        out_ref[tick, block, :, 128 * j : 128 * j + 128] = hidden.astype(BF16)
                        if tick + 1 < ticks:
                            for i in range(width // 8):
                                pieces[tick, 2 * i + j, block] = hidden[
                                    8 * i : 8 * i + 8
                                ].astype(BF16)
                return carry

            lax.fori_loop(0, span // TOGETHER, some_blocks, 0)

            if tick + 1 < ticks:
                for step in order + [0]:
                    other = other_at(step)
                    pltpu.make_async_remote_copy(
                        src_ref=pieces.at[tick, other, group],
                        dst_ref=held[tick + 1].at[
                            pl.ds(owner * per_owner + batch * span, span)
                        ],
                        send_sem=one_send.at[tick + 1],
                        recv_sem=one_recv.at[tick + 1],
                        device_id={"frame": ahead, "tile": other},
                        device_id_type=MESH,
                    ).start()

    sent = first_ref.at[pl.ds(0, tiles - 1)]
    pltpu.make_async_copy(sent, sent, one_send.at[0]).wait()
    for tick in range(ticks):
        if tick + 1 < ticks:
            sent = pieces.at[tick]
            pltpu.make_async_copy(sent, sent, one_send.at[tick + 1]).wait()
        for batch in range(BATCHES):
            sent = picked.at[tick, pl.ds(0, tiles - 1), pl.ds(batch * span, span)]
            pltpu.make_async_copy(sent, sent, two_send.at[tick, batch]).wait()


def stacked_weight(weight):
    out_width, columns = weight.shape
    taps = weight.reshape(out_width, 3, 3, columns // 9)
    return jnp.transpose(taps, (2, 0, 1, 3))


def per_device(frames, state_in, motion, merge_w, res_w, tiles, sections):
    ticks, width, per_owner, pixels = frames.shape[1:]
    first = state_in[0].reshape(width // 8, 8, per_owner, 2, 128)
    first = jnp.transpose(first, (0, 3, 2, 1, 4)).reshape(tiles, per_owner, 8, 128)
    blocks = jnp.transpose(frames[0], (0, 2, 1, 3))
    merge = stacked_weight(merge_w).reshape(3 * width, 3, 2, width)
    merge = jnp.transpose(merge, (0, 2, 1, 3)).reshape(3 * width, 6 * width)
    weight = jnp.stack([stacked_weight(res_w[0, 0]), stacked_weight(res_w[0, 1])])
    weight = weight.reshape(2, 3 * width, 3 * width)
    vmem = pl.BlockSpec(memory_space=pltpu.VMEM)
    piece = (per_owner, 8, 128)
    out = pl.pallas_call(
        functools.partial(kernel, tiles, sections, ticks),
        out_shape=jax.ShapeDtypeStruct((ticks, per_owner, width, pixels), BF16),
        in_specs=[pl.BlockSpec(memory_space=pl.ANY), vmem, vmem, vmem, vmem],
        out_specs=vmem,
        scratch_shapes=[
            pltpu.SMEM((3, ticks, tiles * per_owner), jnp.int32),
            pltpu.VMEM((ticks - 1, tiles) + piece, BF16),
            pltpu.VMEM((tiles * per_owner, 8, 128), BF16),
            pltpu.VMEM((tiles * per_owner, 8, 128), BF16),
            pltpu.VMEM((tiles * per_owner, 8, 128), BF16),
            pltpu.VMEM((ticks, tiles) + piece, BF16),
            pltpu.VMEM((ticks, tiles) + piece, BF16),
            pltpu.VMEM((ticks, per_owner, 3 * width, pixels), BF16),
            pltpu.SemaphoreType.DMA(()),
            pltpu.SemaphoreType.DMA((ticks,)),
            pltpu.SemaphoreType.DMA((ticks,)),
            pltpu.SemaphoreType.DMA((ticks, BATCHES)),
            pltpu.SemaphoreType.DMA((ticks, BATCHES)),
        ],
        compiler_params=pltpu.CompilerParams(
            collective_id=0, has_side_effects=True, vmem_limit_bytes=40 << 20
        ),
    )(motion, first, blocks, merge, weight)
    return jnp.transpose(out, (0, 2, 1, 3))[None]


def solution(mesh):
    placed = (P("frame", None, None, "tile", None), P("frame", None, "tile", None), P(), P(), P())
    body = functools.partial(
        per_device, tiles=mesh.shape["tile"], sections=mesh.shape["frame"]
    )
    return jax.shard_map(
        body,
        mesh=mesh,
        in_specs=placed,
        out_specs=P("frame", None, None, "tile", None),
        check_vma=False,
    )
```

```python
import functools

import jax
import jax.numpy as jnp
from jax import lax
from jax.experimental import pallas as pl
from jax.experimental.pallas import tpu as pltpu
from jax.sharding import PartitionSpec as P

BW = 32
MESH = pl.DeviceIdType.MESH
F32, BF16 = jnp.float32, jnp.bfloat16
BATCHES = 4
TOGETHER = 4


def row_taps(halves, lane):
    low, high = halves
    down_low, down_high = pltpu.roll(low, BW, 1), pltpu.roll(high, BW, 1)
    up_low, up_high = pltpu.roll(low, 128 - BW, 1), pltpu.roll(high, 128 - BW, 1)
    first, last = lane < BW, lane >= 128 - BW
    zero = jnp.zeros_like(low)
    left = jnp.concatenate(
        [jnp.where(first, zero, down_low), low, jnp.where(last, up_high, up_low)], axis=0
    )
    right = jnp.concatenate(
        [jnp.where(first, down_low, down_high), high, jnp.where(last, zero, up_high)], axis=0
    )
    return jnp.concatenate([left, right], axis=1)


def column_sum(product, width, col):
    halves = []
    for half in range(2):
        part = product[:, 128 * half : 128 * half + 128]
        before = jnp.where(col > 0, pltpu.roll(part[:width], 1, 1), 0.0)
        after = jnp.where(col < BW - 1, pltpu.roll(part[2 * width :], 127, 1), 0.0)
        halves.append(before + part[width : 2 * width] + after)
    return halves


def kernel(
    tiles, sections, ticks, motion_ref, first_ref, frames_ref, merge_w_ref, res_w_ref, out_ref,
    moves, turned_moves, merge_ref, weight_ref, pieces, held_0, held_1, held_2, picked, arrived, part,
    moves_sem, turned_sem, one_send, one_recv, two_send, two_recv,
):
    held = (held_0, held_1, held_2)
    section = lax.axis_index("frame")
    owner = lax.axis_index("tile")
    ahead = lax.rem(section + 1, sections)
    behind = lax.rem(section + sections - 1, sections)
    per_owner = pieces.shape[2]
    width = out_ref.shape[2]
    span = per_owner // BATCHES

    moves_copy = pltpu.make_async_copy(motion_ref.at[:, section], moves, moves_sem)
    moves_copy.start()
    odd = lax.rem(owner, 2)
    turned = lax.rem(section + odd, sections)
    turned_copy = pltpu.make_async_copy(motion_ref.at[:, turned], turned_moves, turned_sem)
    turned_copy.start()

    barrier = pltpu.get_barrier_semaphore()

    @pl.loop(1, tiles)
    def _(step):
        pl.semaphore_signal(
            barrier, inc=1, device_id={"tile": lax.rem(owner + step, tiles)}, device_id_type=MESH
        )

    @pl.loop(0, tiles)
    def _(step):
        pl.semaphore_signal(
            barrier, inc=1, device_id={"frame": behind, "tile": step}, device_id_type=MESH
        )

    pl.semaphore_wait(barrier, 2 * tiles - 1)

    order = sorted(range(1, tiles), key=lambda step: -min(step, tiles - step))

    def other_at(step):
        return lax.rem(owner + step, tiles)

    lane = lax.broadcasted_iota(jnp.int32, (width, 128), 1)
    col = lax.rem(lane, BW)

    mine = pl.ds(owner * per_owner, per_owner)
    for step in order:
        other = other_at(step)
        pltpu.make_async_remote_copy(
            src_ref=first_ref.at[other], dst_ref=held[0].at[mine],
            send_sem=one_send.at[0], recv_sem=one_recv.at[0],
            device_id={"tile": other}, device_id_type=MESH,
        ).start()
    held[0][mine] = first_ref[owner]

    for right in range(3):
        rows = pl.ds(right * width, width)
        for down in range(3):
            tap = 3 * down + right
            merge_ref[rows, pl.ds(2 * width * down, 2 * width)] = merge_w_ref[
                :, pl.ds(2 * width * tap, 2 * width)
            ]
        for layer in range(2):
            weight_ref[layer, rows] = jnp.concatenate(
                [
                    res_w_ref[0, layer, :, pl.ds(width * (3 * down + right), width)]
                    for down in range(3)
                ],
                axis=1,
            )

    def frame_taps(turn, carry):
        for tick in range(ticks):
            value = frames_ref[tick, turn]
            part[tick, turn] = row_taps((value[:, :128], value[:, 128:]), lane)
        return carry

    lax.fori_loop(0, per_owner, frame_taps, 0)

    for tick in range(ticks):
        if tick == 0:
            moves_copy.wait()
            turned_copy.wait()
        landed = held[tick].at[pl.ds(0, (tiles - (tick == 0)) * per_owner)]
        pltpu.make_async_copy(landed, landed, one_recv.at[tick]).wait()

        source_of = turned_moves if tick else moves
        for batch in range(BATCHES):
            group = pl.ds(batch * span, span)
            for step in order + [0]:
                other = other_at(step)
                for slot in range(batch * span, batch * span + span):
                    picked[tick, other, slot] = held[tick][
                        source_of[0, tick, other * per_owner + slot]
                    ]

                def send(other=other, tick=tick, batch=batch, group=group):
                    pltpu.make_async_remote_copy(
                        src_ref=picked.at[tick, other, group],
                        dst_ref=arrived.at[tick, owner, group],
                        send_sem=two_send.at[tick, batch], recv_sem=two_recv.at[tick, batch],
                        device_id={"frame": turned if tick else section, "tile": other},
                        device_id_type=MESH,
                    ).start()

                def keep(tick=tick, batch=batch, group=group):
                    pltpu.make_async_copy(
                        picked.at[tick, owner, group], arrived.at[tick, owner, group],
                        two_recv.at[tick, batch],
                    ).start()

                if step:
                    send()
                elif tick:
                    pl.when(odd == 1)(send)
                    pl.when(odd == 0)(keep)
                else:
                    keep()

        for batch in range(BATCHES):
            group = pl.ds(batch * span, span)
            landed = arrived.at[tick, :, group]
            pltpu.make_async_copy(landed, landed, two_recv.at[tick, batch]).wait()

            def some_blocks(turn, carry, tick=tick, batch=batch):
                blocks = [batch * span + turn * TOGETHER + local for local in range(TOGETHER)]

                def displaced(block):
                    down_by = moves[1, tick, owner * per_owner + block]
                    right_by = moves[2, tick, owner * per_owner + block]
                    offset = down_by * BW + right_by
                    col_at = col + right_by
                    turned = [
                        pltpu.roll(
                            jnp.concatenate(
                                [
                                    arrived[tick, 2 * i + j, block].astype(F32)
                                    for i in range(width // 8)
                                ],
                                axis=0,
                            ),
                            lax.rem(3 * 128 - offset, 128),
                            1,
                        ).astype(BF16)
                        for j in range(2)
                    ]
                    halves = []
                    for j in range(2):
                        source = lane + (128 * j + offset)
                        column = (col_at >= 0) & (col_at < BW)
                        from_low = column & (source >= 0) & (source < 128)
                        from_high = column & (source >= 128) & (source < 256)
                        rest = jnp.where(from_high, turned[1], jnp.zeros_like(turned[1]))
                        halves.append(jnp.where(from_low, turned[0], rest))
                    return halves

                def convolved(index, halves):
                    return jnp.dot(
                        weight_ref[index], row_taps(halves, lane), preferred_element_type=F32
                    )

                def merging(block, halves):
                    moved = row_taps(halves, lane)
                    return jnp.dot(
                        merge_ref[...],
                        jnp.concatenate(
                            [
                                taps[width * down : width * (down + 1)]
                                for down in range(3)
                                for taps in (part[tick, block], moved)
                            ],
                            axis=0,
                        ),
                        preferred_element_type=F32,
                    )

                values = [displaced(block) for block in blocks]
                merged = [
                    [
                        jnp.where(half > 0, half, 0.1 * half).astype(BF16)
                        for half in column_sum(merging(block, halves), width, col)
                    ]
                    for block, halves in zip(blocks, values)
                ]
                middle = [
                    [
                        jnp.maximum(half, 0.0).astype(BF16)
                        for half in column_sum(convolved(0, halves), width, col)
                    ]
                    for halves in merged
                ]
                for block, before, halves in zip(blocks, merged, middle):
                    added = column_sum(convolved(1, halves), width, col)
                    for j in range(2):
                        hidden = before[j].astype(F32) + added[j]
                        out_ref[tick, block, :, 128 * j : 128 * j + 128] = hidden.astype(BF16)
                        if tick + 1 < ticks:
                            for i in range(width // 8):
                                pieces[tick, 2 * i + j, block] = hidden[
                                    8 * i : 8 * i + 8
                                ].astype(BF16)
                return carry

            lax.fori_loop(0, span // TOGETHER, some_blocks, 0)

            if tick + 1 < ticks:
                for step in order + [0]:
                    other = other_at(step)
                    target = pl.ds(owner * per_owner + batch * span, span)

                    def send(other=other, tick=tick, group=group, target=target):
                        pltpu.make_async_remote_copy(
                            src_ref=pieces.at[tick, other, group],
                            dst_ref=held[tick + 1].at[target],
                            send_sem=one_send.at[tick + 1],
                            recv_sem=one_recv.at[tick + 1],
                            device_id={
                                "frame": lax.rem(section + 1 - lax.rem(other, 2), sections),
                                "tile": other,
                            },
                            device_id_type=MESH,
                        ).start()

                    def keep(tick=tick, group=group, target=target):
                        pltpu.make_async_copy(
                            pieces.at[tick, owner, group], held[tick + 1].at[target],
                            one_recv.at[tick + 1],
                        ).start()

                    if step:
                        send()
                    else:
                        pl.when(odd == 0)(send)
                        pl.when(odd == 1)(keep)

    def drained(source, count, sem, *rest):
        sent = source.at[(*rest[:1], pl.ds(0, count), *rest[1:])]
        pltpu.make_async_copy(sent, sent, sem).wait()

    drained(first_ref, tiles - 1, one_send.at[0])
    for tick in range(ticks):
        for batch in range(BATCHES):
            group = pl.ds(batch * span, span)
            if tick == 0:
                drained(picked, tiles - 1, two_send.at[tick, batch], tick, group)
                continue
            for parity, count in ((0, tiles - 1), (1, tiles)):
                @pl.when(odd == parity)
                def _(tick=tick, batch=batch, group=group, count=count):
                    drained(picked, count, two_send.at[tick, batch], tick, group)
        if tick + 1 < ticks:
            for parity, count in ((0, tiles), (1, tiles - 1)):
                @pl.when(odd == parity)
                def _(tick=tick, count=count):
                    drained(pieces, count, one_send.at[tick + 1], tick)


def per_device(frames, state_in, motion, merge_w, res_w, tiles, sections):
    ticks, width, per_owner, pixels = frames.shape[1:]
    first = state_in[0].reshape(width // 8, 8, per_owner, 2, 128)
    first = jnp.transpose(first, (0, 3, 2, 1, 4)).reshape(tiles, per_owner, 8, 128)
    blocks = jnp.transpose(frames[0], (0, 2, 1, 3))
    vmem = pl.BlockSpec(memory_space=pltpu.VMEM)
    piece = (per_owner, 8, 128)
    out = pl.pallas_call(
        functools.partial(kernel, tiles, sections, ticks),
        out_shape=jax.ShapeDtypeStruct((ticks, per_owner, width, pixels), BF16),
        in_specs=[pl.BlockSpec(memory_space=pl.ANY), vmem, vmem, vmem, vmem],
        out_specs=vmem,
        scratch_shapes=[
            pltpu.SMEM((3, ticks, tiles * per_owner), jnp.int32),
            pltpu.SMEM((3, ticks, tiles * per_owner), jnp.int32),
            pltpu.VMEM((3 * width, 6 * width), BF16),
            pltpu.VMEM((2, 3 * width, 3 * width), BF16),
            pltpu.VMEM((ticks - 1, tiles) + piece, BF16),
            pltpu.VMEM((tiles * per_owner, 8, 128), BF16),
            pltpu.VMEM((tiles * per_owner, 8, 128), BF16),
            pltpu.VMEM((tiles * per_owner, 8, 128), BF16),
            pltpu.VMEM((ticks, tiles) + piece, BF16),
            pltpu.VMEM((ticks, tiles) + piece, BF16),
            pltpu.VMEM((ticks, per_owner, 3 * width, pixels), BF16),
            pltpu.SemaphoreType.DMA(()),
            pltpu.SemaphoreType.DMA(()),
            pltpu.SemaphoreType.DMA((ticks,)),
            pltpu.SemaphoreType.DMA((ticks,)),
            pltpu.SemaphoreType.DMA((ticks, BATCHES)),
            pltpu.SemaphoreType.DMA((ticks, BATCHES)),
        ],
        compiler_params=pltpu.CompilerParams(
            collective_id=0, has_side_effects=True, vmem_limit_bytes=40 << 20
        ),
    )(motion, first, blocks, merge_w, res_w)
    return jnp.transpose(out, (0, 2, 1, 3))[None]


def solution(mesh):
    placed = (P("frame", None, None, "tile", None), P("frame", None, "tile", None), P(), P(), P())
    body = functools.partial(
        per_device, tiles=mesh.shape["tile"], sections=mesh.shape["frame"]
    )
    return jax.shard_map(
        body,
        mesh=mesh,
        in_specs=placed,
        out_specs=P("frame", None, None, "tile", None),
        check_vma=False,
    )
```
